32 devices in a mesh: row: 2 (over y), col: 4 (over x, core), layer: 4 (over z).
Axes of the slice: x: 2, y: 2, z: 4, core: 2. Of those that a mesh axis runs over, the one named last changes fastest.
Arguments:
- left: float32 [1024, 8192], P('row', ('layer', 'col')), may hold values from -6 to 6
- right: float32 [8192, 16384], P(('layer', 'row'), 'col'), may hold values from -0.125 to 0.125
- left_mask: int32 [2, 16], replicated, may hold values 0 or 1
- right_mask: int32 [16, 32], replicated, may hold values 0 or 1
- result_mask: int32 [2, 32], replicated, may hold values 0 or 1
Outputs:
- ladder: float32 [1024, 16384], P('row', ('col', 'layer'))
The draws below stay inside these ranges and needn't reach their ends.
Inputs may be any that keep to these rules, and one draw needn't show every extreme that they name: `left_mask`: 1 marks a present tile, 0 an absent one. `right_mask`: 1 marks a present tile, 0 an absent one. `result_mask`: 1 marks a present tile, 0 an absent one.
All inputs are finite; a program needn't handle non-finite values.
Results may differ from the reference program's by a relative error of at most 0.0003.
Values sent between devices are 32-bit elements; how exact they have to be, the bound alone decides.
A program may use at most 128 MiB of HBM per device.

```python
import jax
import jax.numpy as jnp
from jax import lax

K = 8192
N = 16384
TILE = 512
M = 1024
MT = 2
KT = 16
NT = 32


def place_ends(array, stream_key, low, largest):
    longest = array.shape.index(max(array.shape))
    spots = []
    for shift in (0, 1):
        where = [jax.random.randint(jax.random.fold_in(stream_key, axis), (), 0, length) for axis, length in enumerate(array.shape)]
        where[longest] = (where[longest] + shift) % array.shape[longest]
        spots.append(tuple(where))
    return array.at[spots[0]].set(low).at[spots[1]].set(largest)


def shard_levels(own_key, shape, shards, low, top_value):
    loudness = 1.0
    for dim, parts in shards:
        heights = jax.random.uniform(jax.random.fold_in(jax.random.fold_in(own_key, 6), dim), (parts,), jnp.float32, low / len(shards), top_value / len(shards))
        loudness = loudness * jnp.repeat(jnp.exp(heights), shape[dim] // parts).reshape((-1,) + (1,) * (len(shape) - 1 - dim))
    return loudness


def gaussian(key, extent, spread, bound, pieces=(), kind=jnp.bfloat16):
    loudness = shard_levels(key, extent, pieces, -0.22, 0.18) if pieces else 1.0
    result = jax.random.normal(key, extent, jnp.float32) * spread * loudness
    return jnp.minimum(jnp.maximum(result, -bound), bound).astype(kind)


def setup_inputs(seed: int = 0) -> dict:
    arg_keys = jax.random.split(jax.random.key(seed), 6)
    left = gaussian(arg_keys[0], (M, K), 1.0, 6.0, ((0, 2), (1, 16)), jnp.float32)
    right = gaussian(arg_keys[1], (K, N), (K // 4) ** -0.5, 0.125, ((0, 8), (1, 4)), jnp.float32)
    left_mask = place_ends((jax.random.randint(arg_keys[2], (MT, KT), 0, 2) < 1).astype(jnp.int32), jax.random.fold_in(arg_keys[2], 1), 0, 1)
    right_mask = place_ends((jax.random.randint(arg_keys[3], (KT, NT), 0, 2) < 1).astype(jnp.int32), jax.random.fold_in(arg_keys[3], 1), 0, 1)
    result_mask = place_ends((jax.random.randint(arg_keys[4], (MT, NT), 0, 2) < 1).astype(jnp.int32), jax.random.fold_in(arg_keys[4], 1), 0, 1)
    return dict(left=left, right=right, left_mask=left_mask, right_mask=right_mask, result_mask=result_mask)


def reference(left, right, left_mask, right_mask, result_mask):
    rows_total = left.shape[0]
    tile_rows = left_mask.shape[0]
    tile_inner = right_mask.shape[0]
    tile_cols = right_mask.shape[1]
    padded = jnp.pad(left, ((0, tile_rows * TILE - rows_total), (0, 0)))

    def column(jcol):
        def per_row(irow):
            def step(kidx, total):
                kpos = jnp.asarray(kidx).astype(jnp.int32)
                usable = (left_mask[irow, kpos] * right_mask[kpos, jcol] * result_mask[irow, jcol]) > 0
                block_a = lax.dynamic_slice(padded, ((irow * TILE).astype(jnp.int32), (kpos * TILE).astype(jnp.int32)), (TILE, TILE))
                block_b = lax.dynamic_slice(right, ((kpos * TILE).astype(jnp.int32), (jcol * TILE).astype(jnp.int32)), (TILE, TILE))
                return lax.cond(usable, lambda acc: acc + jnp.dot(block_a, block_b, precision=lax.Precision.HIGHEST), lambda acc: acc, total)
            return lax.fori_loop(0, tile_inner, step, jnp.zeros((TILE, TILE), left.dtype))
        return lax.map(per_row, jnp.arange(tile_rows, dtype=jnp.int32))

    blocks = lax.map(column, jnp.arange(tile_cols, dtype=jnp.int32))
    whole = jnp.transpose(blocks, (1, 2, 0, 3)).reshape(tile_rows * TILE, tile_cols * TILE)
    return whole[:rows_total]
```

```python
import functools
import math

import jax
import jax.numpy as jnp
import numpy as np
from jax import lax
from jax.experimental import pallas as pl
from jax.experimental.pallas import tpu as pltpu
from jax.sharding import PartitionSpec as P

TILE = 512
HEAD = 4


def needed_at(layer, owner, layers):
    return layers if owner == layer else layers - 1 - abs(owner - layer)


def owner_order(layer, layers):
    return sorted(range(layers), key=lambda owner: (needed_at(layer, owner, layers), -owner if layer < layers // 2 else owner))


def split(values):
    high = values.astype(jnp.bfloat16)
    return high, (values - high.astype(jnp.float32)).astype(jnp.bfloat16)


def tile_kernel(which, base, added, info, left_mask, right_mask, result_mask, high_ref, low_ref, right_ref, *rest):
    out_ref = rest[-1]
    row = info[which]
    col = info[HEAD + base + pl.program_id(0)]
    width, side = out_ref.shape[2], math.gcd(TILE, right_ref.shape[0])
    col_tile = (info[3] + col) * width // TILE
    out_ref[...] = rest[0][...] if added else jnp.zeros_like(out_ref)
    for step in range(right_ref.shape[0] // side):
        inner = (info[2] + step) * side // TILE
        usable = left_mask[row, inner] * right_mask[inner, col_tile] * result_mask[row, col_tile]

        @pl.when(usable > 0)
        def _():
            at = pl.ds(step * side, side)
            high, low = split(right_ref[at, :])
            left_high, left_low = high_ref[:, at], low_ref[:, at]
            dot = functools.partial(jnp.dot, preferred_element_type=jnp.float32)
            out_ref[0] += dot(left_high, low) + dot(left_low, high) + dot(left_high, high)


def tiles(which, base, count, width, tables, left_parts, right, prev=None):
    rows = left_parts[0].shape[0]
    depth = right.shape[0]
    whole = pl.BlockSpec((rows, depth), lambda s, *_: (0, 0))
    slot = pl.BlockSpec((1, rows, width), lambda s, *_: (s, 0, 0))
    extra = () if prev is None else (prev,)
    return pl.pallas_call(
        functools.partial(tile_kernel, which, base, prev is not None),
        grid_spec=pltpu.PrefetchScalarGridSpec(
            num_scalar_prefetch=4,
            grid=(count,),
            in_specs=[whole, whole, pl.BlockSpec((depth, width), lambda s, info, *_: (0, info[HEAD + base + s]))]
            + [slot] * len(extra),
            out_specs=slot,
        ),
        out_shape=jax.ShapeDtypeStruct((count, rows, width), jnp.float32),
        cost_estimate=pl.CostEstimate(
            flops=6 * count * rows * depth * width,
            bytes_accessed=4 * count * width * (depth + 2 * rows) + 4 * rows * depth,
            transcendentals=0,
        ),
    )(*tables, *left_parts, right, *extra)


def pick(position, choices):
    value = choices[-1][1]
    for where, array in choices[:-1]:
        value = jnp.where(position == where, array, value)
    return value


def shards(layers, left, right, left_mask, right_mask, result_mask):
    rows, left_cols = left.shape
    depth, cols = right.shape
    row_count, col_count = lax.axis_size("row"), lax.axis_size("col")
    row, col, layer = lax.axis_index("row"), lax.axis_index("col"), lax.axis_index("layer")
    group = col_count // row_count
    width = math.gcd(TILE, cols // layers)
    per_chunk = cols // layers // width

    def send(value, axes, pairs):
        return lax.ppermute(value, axes, pairs)

    parts = []
    for shift in range(row_count):
        pairs = []
        for to_row in range(row_count):
            for to_col in range(col_count):
                source = ((to_col // group + shift) % row_count, to_row * group + to_col % group)
                pairs.append((source[0] * col_count + source[1], to_row * col_count + to_col))
        parts.append(send(left, ("row", "col"), pairs))
    col_group, member = col // group, col % group
    mine_first = col_group == row
    ordered = jnp.stack([jnp.where(mine_first, parts[0], parts[1]), jnp.where(mine_first, parts[1], parts[0])])
    blocks = [ordered]
    for shift in range(1, group):
        pairs = [
            (c // group * group + (c % group + shift) % group, c) for c in range(col_count)
        ]
        blocks.append(send(ordered, "col", pairs))
    placed = []
    for place in range(group):
        block = blocks[0]
        for shift in range(1, group):
            block = jnp.where((member + shift) % group == place, blocks[shift], block)
        placed.append(block)
    joined = jnp.concatenate(placed, axis=2)
    rounded = lax.reduce_precision(joined, 8, 7)
    high, low = rounded.astype(jnp.bfloat16), (joined - rounded).astype(jnp.bfloat16)
    left_mine, left_other = (high[0], low[0]), (high[1], low[1])

    orders = np.array([[owner * per_chunk + t for owner in owner_order(l, layers) for t in range(per_chunk)] for l in range(layers)], np.int32)
    head = jnp.stack([row, row_count - 1 - row, (layer * row_count + row) * (depth // math.gcd(TILE, depth)), col * (cols // width)])
    info = jnp.concatenate([head.astype(jnp.int32), jnp.asarray(orders)[layer]])
    tables = (info, left_mask, right_mask, result_mask)

    swap = [(r, row_count - 1 - r) for r in range(row_count)]
    outgoing = [tiles(1, p * per_chunk, per_chunk, width, tables, left_other, right) for p in range(layers)]
    incoming = [send(value, "row", swap) for value in outgoing]
    sums = [tiles(0, p * per_chunk, per_chunk, width, tables, left_mine, right, incoming[p]) for p in range(layers)]

    up = down = None
    for step in range(layers - 1):
        arrived = []
        for sign, carried in ((1, up), (-1, down)):
            active = [l for l in range(layers) if 0 <= l + sign * (layers - 1 - step) < layers]
            position = {l: owner_order(l, layers).index(l + sign * (layers - 1 - step)) for l in active}
            used = sorted(set(position.values()))
            lookup = jnp.asarray(np.array([position.get(l, used[0]) for l in range(layers)], np.int32))[layer] if len(used) > 1 else 0
            value = pick(lookup, [(p, sums[p]) for p in used])
            if carried is not None:
                value = value + carried
            arrived.append(send(value, "layer", [(l, l + sign) for l in active]))
        up, down = arrived
    total = sums[layers - 1] + up + down
    return jnp.concatenate([total[t] for t in range(per_chunk)], axis=1)


def solution(mesh):
    placed = (P("row", ("layer", "col")), P(("layer", "row"), "col"), P(), P(), P())
    return jax.shard_map(
        functools.partial(shards, mesh.shape["layer"]),
        mesh=mesh,
        in_specs=placed,
        out_specs=P("row", ("col", "layer")),
        check_vma=False,
    )
```

```python
import functools
import math

import jax
import jax.numpy as jnp
import numpy as np
from jax import lax
from jax.experimental import pallas as pl
from jax.experimental.pallas import tpu as pltpu
from jax.sharding import PartitionSpec as P

TILE = 512
HEAD = 4


def needed_at(layer, owner, layers):
    return layers if owner == layer else layers - 1 - abs(owner - layer)


def owner_order(layer, layers):
    return sorted(range(layers), key=lambda owner: (needed_at(layer, owner, layers), -owner if layer < layers // 2 else owner))


def split(values):
    high = values.astype(jnp.bfloat16)
    return high, (values - high.astype(jnp.float32)).astype(jnp.bfloat16)


def tile_kernel(which, slot, places, added, info, left_mask, right_mask, result_mask, *refs):
    left_refs, right_ref, out_ref = refs[: 2 * places], refs[2 * places], refs[-1]
    row = info[which]
    depth, width = right_ref.shape[0] // places, out_ref.shape[1]
    col_tile = (info[3] + info[HEAD + slot]) * width // TILE
    out_ref[...] = refs[2 * places + 1][...] if added else jnp.zeros_like(out_ref)
    for place in range(places):
        inner = (info[2] + place) * depth // TILE
        usable = left_mask[row, inner] * right_mask[inner, col_tile] * result_mask[row, col_tile]

        @pl.when(usable > 0)
        def _():
            high, low = split(right_ref[pl.ds(place * depth, depth), :])
            left_high, left_low = left_refs[2 * place][...], left_refs[2 * place + 1][...]
            dot = functools.partial(jnp.dot, preferred_element_type=jnp.float32)
            out_ref[...] += dot(left_high, low) + dot(left_low, high) + dot(left_high, high)


def tile(which, slot, width, tables, left_parts, right, prev=None):
    rows, part = left_parts[0].shape
    depth = right.shape[0]
    piece = pl.BlockSpec((rows, part), lambda s, *_: (0, 0))
    whole = pl.BlockSpec((rows, width), lambda s, *_: (0, 0))
    extra = () if prev is None else (prev,)
    return pl.pallas_call(
        functools.partial(tile_kernel, which, slot, len(left_parts) // 2, prev is not None),
        grid_spec=pltpu.PrefetchScalarGridSpec(
            num_scalar_prefetch=4,
            grid=(1,),
            in_specs=[piece] * len(left_parts)
            + [pl.BlockSpec((depth, width), lambda s, info, *_: (0, info[HEAD + slot]))]
            + [whole] * len(extra),
            out_specs=whole,
        ),
        out_shape=jax.ShapeDtypeStruct((rows, width), jnp.float32),
        cost_estimate=pl.CostEstimate(
            flops=6 * rows * depth * width,
            bytes_accessed=4 * width * (depth + 2 * rows) + 4 * rows * depth,
            transcendentals=0,
        ),
    )(*tables, *left_parts, right, *extra)


def pick(position, choices):
    value = choices[-1][1]
    for where, array in choices[:-1]:
        value = jnp.where(position == where, array, value)
    return value


def shards(layers, left, right, left_mask, right_mask, result_mask):
    rows, left_cols = left.shape
    depth, cols = right.shape
    row_count, col_count = lax.axis_size("row"), lax.axis_size("col")
    row, col, layer = lax.axis_index("row"), lax.axis_index("col"), lax.axis_index("layer")
    group = col_count // row_count
    width = math.gcd(TILE, cols // layers)
    per_chunk = cols // layers // width

    def send(value, axes, pairs):
        return lax.ppermute(value, axes, pairs)

    parts = []
    for shift in range(row_count):
        pairs = []
        for to_row in range(row_count):
            for to_col in range(col_count):
                source = ((to_col // group + shift) % row_count, to_row * group + to_col % group)
                pairs.append((source[0] * col_count + source[1], to_row * col_count + to_col))
        parts.append(send(left, ("row", "col"), pairs))
    col_group, member = col // group, col % group
    pieces = [parts]
    for shift in range(1, group):
        pairs = [(c // group * group + (c % group + shift) % group, c) for c in range(col_count)]
        pieces.append([send(part, "col", pairs) for part in parts])
    left_mine, left_other = [], []
    for target, chosen in ((row, left_mine), (row_count - 1 - row, left_other)):
        turn = (target - col_group) % row_count
        for place in range(group):
            value = pick((place - member) % group * row_count + turn, [(u * row_count + t, pieces[u][t]) for u in range(group) for t in range(row_count)])
            rounded = lax.reduce_precision(value, 8, 7)
            chosen += [rounded.astype(jnp.bfloat16), (value - rounded).astype(jnp.bfloat16)]

    orders = np.array([[owner * per_chunk + t for owner in owner_order(l, layers) for t in range(per_chunk)] for l in range(layers)], np.int32)
    head = jnp.stack([row, row_count - 1 - row, (layer * row_count + row) * group, col * (cols // width)])
    info = jnp.concatenate([head.astype(jnp.int32), jnp.asarray(orders)[layer]])
    tables = (info, left_mask, right_mask, result_mask)

    swap = [(r, row_count - 1 - r) for r in range(row_count)]
    slots = range(layers * per_chunk)
    incoming = [send(tile(1, slot, width, tables, left_other, right), "row", swap) for slot in slots]
    sums = [tile(0, slot, width, tables, left_mine, right, incoming[slot]) for slot in slots]

    carried = {}
    for step in range(layers - 1):
        for t in range(per_chunk):
            for sign in (1, -1):
                active = [l for l in range(layers) if 0 <= l + sign * (layers - 1 - step) < layers]
                position = {l: owner_order(l, layers).index(l + sign * (layers - 1 - step)) for l in active}
                used = sorted(set(position.values()))
                lookup = 0
                for p in used:
                    for l in active:
                        lookup = lookup + jnp.where(layer == l, p, 0) if position[l] == p else lookup
                value = pick(lookup, [(p, sums[p * per_chunk + t]) for p in used])
                if step:
                    value = value + carried[sign, t]
                carried[sign, t] = send(value, "layer", [(l, l + sign) for l in active])
    last = (layers - 1) * per_chunk
    return jnp.concatenate([sums[last + t] + carried[1, t] + carried[-1, t] for t in range(per_chunk)], axis=1)


def solution(mesh):
    placed = (P("row", ("layer", "col")), P(("layer", "row"), "col"), P(), P(), P())
    return jax.shard_map(
        functools.partial(shards, mesh.shape["layer"]),
        mesh=mesh,
        in_specs=placed,
        out_specs=P("row", ("col", "layer")),
        check_vma=False,
    )
```

```python
import functools
import math

import jax
import jax.numpy as jnp
import numpy as np
from jax import lax
from jax.experimental import pallas as pl
from jax.experimental.pallas import tpu as pltpu
from jax.sharding import PartitionSpec as P

TILE = 512
HEAD = 4


def needed_at(layer, owner, layers):
    return layers if owner == layer else layers - 1 - abs(owner - layer)


def owner_order(layer, layers):
    return sorted(range(layers), key=lambda owner: (needed_at(layer, owner, layers), -owner if layer < layers // 2 else owner))


def split(values):
    high = values.astype(jnp.bfloat16)
    return high, (values - high.astype(jnp.float32)).astype(jnp.bfloat16)


def tile_kernel(which, slot, places, sources, info, left_mask, right_mask, result_mask, *refs):
    left_refs, right_ref = refs[: 2 * places], refs[2 * places]
    out_ref, high_ref, low_ref = refs[-3:]
    row = info[which]
    depth, width = right_ref.shape[0] // places, out_ref.shape[1]
    col_tile = (info[3] + info[HEAD + slot]) * width // TILE
    out_ref[...] = jnp.zeros_like(out_ref)
    incoming = refs[2 * places + 1 : 2 * places + 1 + sources]
    for source, ref in enumerate(incoming):

        @pl.when(info[HEAD + slot + (info.shape[0] - HEAD) // 3] == source)
        def _():
            pltpu.sync_copy(ref, out_ref)

    for place in range(places):
        inner = (info[2] + place) * depth // TILE
        usable = left_mask[row, inner] * right_mask[inner, col_tile] * result_mask[row, col_tile]

        @pl.when(usable > 0)
        def _():
            high_ref[...], low_ref[...] = split(right_ref[pl.ds(place * depth, depth), :])
            some = math.gcd(out_ref.shape[0], 256)

            @pl.loop(0, out_ref.shape[0] // some)
            def _(block):
                at = pl.ds(pl.multiple_of(block * some, some), some)
                left_high, left_low = left_refs[2 * place][at, :], left_refs[2 * place + 1][at, :]
                dot = functools.partial(jnp.dot, preferred_element_type=jnp.float32)
                out_ref[at, :] += dot(left_high, low_ref[...]) + dot(left_low, high_ref[...]) + dot(left_high, high_ref[...])


def tile(which, slot, width, tables, left_parts, right, incoming=(), after=()):
    rows, part = left_parts[0].shape
    depth = right.shape[0]
    piece = pl.BlockSpec((rows, part), lambda s, *_: (0, 0))
    whole = pl.BlockSpec((rows, width), lambda s, *_: (0, 0))
    return pl.pallas_call(
        functools.partial(tile_kernel, which, slot, len(left_parts) // 2, len(incoming)),
        grid_spec=pltpu.PrefetchScalarGridSpec(
            num_scalar_prefetch=4,
            grid=(1,),
            in_specs=[piece] * len(left_parts)
            + [pl.BlockSpec((depth, width), lambda s, info, *_: (0, info[HEAD + slot]))]
            + [pl.BlockSpec(memory_space=pl.ANY)] * (len(incoming) + len(after)),
            out_specs=whole,
            scratch_shapes=[pltpu.VMEM((part, width), jnp.bfloat16)] * 2,
        ),
        out_shape=jax.ShapeDtypeStruct((rows, width), jnp.float32),
        cost_estimate=pl.CostEstimate(
            flops=6 * rows * depth * width,
            bytes_accessed=4 * width * (depth + 2 * rows) + 4 * rows * depth,
            transcendentals=0,
        ),
    )(*tables, *left_parts, right, *incoming, *after)


def pick(position, choices):
    value = choices[-1][1]
    for where, array in choices[:-1]:
        value = jnp.where(position == where, array, value)
    return value


def shards(layers, left, right, left_mask, right_mask, result_mask):
    rows, left_cols = left.shape
    depth, cols = right.shape
    row_count, col_count = lax.axis_size("row"), lax.axis_size("col")
    row, col, layer = lax.axis_index("row"), lax.axis_index("col"), lax.axis_index("layer")
    group = col_count // row_count
    width = math.gcd(TILE, cols // layers)
    per_chunk = cols // layers // width

    def send(value, axes, pairs):
        return lax.ppermute(value, axes, pairs)

    parts = []
    for shift in range(row_count):
        pairs = []
        for to_row in range(row_count):
            for to_col in range(col_count):
                source = ((to_col // group + shift) % row_count, to_row * group + to_col % group)
                pairs.append((source[0] * col_count + source[1], to_row * col_count + to_col))
        parts.append(send(left, ("row", "col"), pairs))
    col_group, member = col // group, col % group
    pieces = [parts]
    for shift in range(1, group):
        pairs = [(c // group * group + (c % group + shift) % group, c) for c in range(col_count)]
        pieces.append([send(part, "col", pairs) for part in parts])
    left_mine, left_other = [], []
    for target, chosen in ((row, left_mine), (row_count - 1 - row, left_other)):
        turn = (target - col_group) % row_count
        for place in range(group):
            value = pick((place - member) % group * row_count + turn, [(u * row_count + t, pieces[u][t]) for u in range(group) for t in range(row_count)])
            rounded = lax.reduce_precision(value, 8, 7)
            chosen += [rounded.astype(jnp.bfloat16), (value - rounded).astype(jnp.bfloat16)]

    orders = np.array([[owner * per_chunk + t for owner in owner_order(l, layers) for t in range(per_chunk)] for l in range(layers)], np.int32)
    head = jnp.stack([row, row_count - 1 - row, (layer * row_count + row) * group, col * (cols // width)])
    order = jnp.asarray(orders)[layer]
    slots = cols // width
    usable = left_mask[:, :, None] * right_mask[None] * result_mask[:, None, :]
    blocks = layers * row_count
    usable = jnp.max(usable.reshape(row_count, blocks, -1, usable.shape[2]), axis=2)
    usable = jnp.repeat(usable, col_count * slots // usable.shape[2], axis=2)
    usable = usable.reshape(row_count, layers, row_count, col_count, slots)
    crossing = jnp.stack([usable[row_count - 1 - r, :, r] for r in range(row_count)])
    most = jnp.max(jnp.sum(crossing, axis=-1))
    ordered = order[:, None] == jnp.arange(slots)[None, :]
    earlier = np.tril(np.ones((slots, slots), np.int32), -1)

    def ranked(sender):
        here = jnp.sum(ordered * crossing[sender, layer, col][None, :], axis=1)
        return here, jnp.sum(earlier * here[None, :], axis=1)

    here, rank = ranked(row)
    packed = jnp.sum((rank[None, :] == jnp.arange(slots)[:, None]) * (here * order)[None, :], axis=1)
    there, place_there = ranked(row_count - 1 - row)
    found = jnp.where(there > 0, place_there, -1)
    info = jnp.concatenate([head, packed, order, found]).astype(jnp.int32)
    tables = (info, left_mask, right_mask, result_mask)

    def rest(sent):
        return finish(layers, per_chunk, width, sent, tables, left_mine, left_other, right, layer, row_count)

    few = slots * 3 // 4
    return lax.cond(most <= few, lambda: rest(few), lambda: rest(slots))


def finish(layers, per_chunk, width, sent, tables, left_mine, left_other, right, layer, row_count):
    def send(value, axes, pairs):
        return lax.ppermute(value, axes, pairs)

    slots = layers * per_chunk
    swap = [(r, row_count - 1 - r) for r in range(row_count)]
    incoming = [send(tile(1, slot, width, tables, left_other, right), "row", swap) for slot in range(sent)]
    sums, carried, after = [], {}, ()
    for slot in range(slots):
        sums.append(tile(0, slots + slot, width, tables, left_mine, right, incoming[: slot + 1], after))
        step, t = divmod(slot, per_chunk)
        if step == layers - 1:
            after = ()
            continue
        values = []
        for sign in (1, -1):
            active = [l for l in range(layers) if 0 <= l + sign * (layers - 1 - step) < layers]
            position = {l: owner_order(l, layers).index(l + sign * (layers - 1 - step)) for l in active}
            used = sorted(set(position.values()))
            lookup = sum(jnp.where(layer == l, position[l], 0) for l in active)
            value = pick(lookup, [(p, sums[p * per_chunk + t]) for p in used])
            if step:
                value = value + carried[sign, t]
            carried[sign, t] = send(value, "layer", [(l, l + sign) for l in active])
            values.append(value)
        after = tuple(values) if step else ()
    last = (layers - 1) * per_chunk
    return jnp.concatenate([sums[last + t] + carried[1, t] + carried[-1, t] for t in range(per_chunk)], axis=1)


def solution(mesh):
    placed = (P("row", ("layer", "col")), P(("layer", "row"), "col"), P(), P(), P())
    return jax.shard_map(
        functools.partial(shards, mesh.shape["layer"]),
        mesh=mesh,
        in_specs=placed,
        out_specs=P("row", ("col", "layer")),
        check_vma=False,
    )
```
